32 devices in a mesh: clip: 2 (over x), slab: 16 (over z, y, core).
Axes of the slice: x: 2, y: 2, z: 4, core: 2. Of those that a mesh axis runs over, the one named last changes fastest.
Arguments:
- mask_field: float32 [4096, 2048], P(('clip', 'slab')), parts along dimension 0, may hold values from -1.8 to 2.9
- target_print: int32 [4096, 2048], P(('clip', 'slab')), parts along dimension 0, may hold values from 0 to 1
- source_points: int32 [32, 2], P('clip'), parts along dimension 0, may hold values from 0 to 60
- source_groups: int32 [32], P('clip'), parts along dimension 0, may hold values from 0 to 7
- group_logits: float32 [16], P('clip'), parts along dimension 0, may hold values from -1 to 1
- pupil_radius: int32 [2], P('clip'), parts along dimension 0, may hold values from 32 to 127
Outputs:
- loss_value: float32 [2], P('clip'), parts along dimension 0
- mask_grad: float32 [4096, 2048], P(('clip', 'slab')), parts along dimension 0
- group_grad: float32 [16], P('clip'), parts along dimension 0
The draws below stay inside these ranges and needn't reach their ends.
There are 2 independent parts, one for each index of `clip`. The reference program is written for one: setup_inputs(seed, part) draws one part's arguments, and reference() takes and returns one part's arrays. A program takes and returns all parts, laid end to end along the dimension named above; each array names one. Nothing has to cross between parts.
All inputs are finite; a program needn't handle non-finite values.
Results may differ from the reference program's by a relative error of at most 0.0003.
Values sent between devices are 32-bit elements; how exact they have to be, the bound alone decides.
A program may use at most 128 MiB of HBM per device.

```python
import math
import jax
import jax.numpy as jnp
from jax import lax

N = 2048
K = 256
GRID = 61
NS = 16
NG = 8


def draw_mask_field(key, part):
    keys = jax.random.split(key, 5)
    rough = jax.random.uniform(keys[0], (N, N), jnp.float32)
    amplitude = jax.random.uniform(keys[1], (16,), jnp.float32, -1.0, 1.0)
    offset = 0.5
    wave_limit = 15 * K // 32
    first_wave = jax.random.randint(keys[2], (16,), -wave_limit, wave_limit + 1)
    second_wave = jax.random.randint(keys[3], (16,), -wave_limit, wave_limit + 1)
    phase_shift = jax.random.uniform(keys[4], (16,), jnp.float32, 0.0, 2.0 * math.pi)
    row_index = jnp.arange(N, dtype=jnp.int32)[:, None]
    col_index = jnp.arange(N, dtype=jnp.int32)[None, :]
    smooth = jnp.zeros((N, N), jnp.float32)
    for member in range(16):
        wrapped = jnp.mod(first_wave[member] * row_index + second_wave[member] * col_index, N)
        angles = 2.0 * math.pi * wrapped.astype(jnp.float32) / N + phase_shift[member]
        smooth = smooth + amplitude[member] * jnp.cos(angles)
    return offset + 0.12 * smooth + 0.3 * (2.0 * rough - 1.0)


def draw_target_print(key, part):
    row_index = jnp.arange(N, dtype=jnp.int32)[:, None]
    numbers = jax.random.randint(key, (N, N), 0, 1000)
    limit = 200 + 600 * row_index // N
    return (numbers < limit).astype(jnp.int32)


def with_ends(values, key, low, top_value):
    longest = values.shape.index(max(values.shape))
    spots = []
    for shift in (0, 1):
        where = [jax.random.randint(jax.random.fold_in(key, axis), (), 0, length) for axis, length in enumerate(values.shape)]
        where[longest] = (where[longest] + shift) % values.shape[longest]
        spots.append(tuple(where))
    return values.at[spots[0]].set(low).at[spots[1]].set(top_value)


def setup_inputs(seed: int = 0, part: int = 0) -> dict:
    key_of = jax.random.split(jax.random.key(seed), 7)
    part_keys = jax.random.split(jax.random.fold_in(key_of[6], part), 7)
    mask_field = draw_mask_field(jax.random.fold_in(jax.random.fold_in(key_of[6], part), 71), part)
    target_print = draw_target_print(jax.random.fold_in(jax.random.fold_in(key_of[6], part), 71), part)
    source_points = with_ends(jax.random.randint(part_keys[2], (NS, 2), 0, GRID), jax.random.fold_in(part_keys[2], 1), 0, GRID - 1).astype(jnp.int32)
    source_groups = with_ends(jax.random.randint(part_keys[3], (NS,), 0, NG), jax.random.fold_in(part_keys[3], 1), 0, NG - 1).astype(jnp.int32)
    group_logits = jnp.clip(jax.random.uniform(part_keys[4], (NG,), jnp.float32, -1.0, 1.0), -1.0, 1.0)
    pupil_radius = jax.random.randint(part_keys[5], (1,), K // 8, K // 2).astype(jnp.int32)
    return {"mask_field": mask_field, "target_print": target_print, "source_points": source_points, "source_groups": source_groups, "group_logits": group_logits, "pupil_radius": pupil_radius}


steepness = 8.0
threshold = 0.3
shift_scale = 45

def reference(mask_field, target_print, source_points, source_groups, group_logits, pupil_radius):
    half_band = K // 2
    frequency = jnp.arange(K, dtype=jnp.int32) - half_band
    band_index = jnp.mod(frequency, N).astype(jnp.int32)
    cutoff = pupil_radius[0].astype(jnp.int32)
    shifted = (source_points.astype(jnp.int32) - GRID // 2) * cutoff // shift_scale
    desired = target_print.astype(mask_field.dtype)

    def objective(field, logits):
        spectrum = jnp.fft.fft2(field)
        band = jnp.take(jnp.take(spectrum, band_index, axis=0), band_index, axis=1)
        weights = jnp.exp(logits[source_groups])
        total_weight = jnp.sum(weights)

        def add_source(running, source_item):
            offset, weight = source_item
            first_axis = frequency[:, None] + offset[0]
            second_axis = frequency[None, :] + offset[1]
            passed = first_axis * first_axis + second_axis * second_axis <= cutoff * cutoff
            clipped = jnp.where(passed, band, jnp.zeros_like(band))
            embedded = jnp.zeros((N, N), band.dtype).at[band_index[:, None], band_index[None, :]].set(clipped)
            image_field = jnp.fft.ifft2(embedded)
            bright = jnp.real(image_field) * jnp.real(image_field) + jnp.imag(image_field) * jnp.imag(image_field)
            return (running + weight * bright, None)
        running, unused = lax.scan(add_source, jnp.zeros((N, N), field.dtype), (shifted, weights))
        intensity = running / total_weight
        resist = jax.nn.sigmoid(steepness * (intensity - threshold))
        misfit = resist - desired
        return jnp.sum(misfit * misfit)
    total_sq, pullback = jax.vjp(objective, mask_field, group_logits)
    mask_grad, logit_grad = pullback(jnp.ones_like(total_sq))
    norming = 1.0 / (N * N)
    return ((total_sq * norming).reshape(1), mask_grad, logit_grad * norming)
```

```python
import functools
import math

import jax
import jax.numpy as jnp
import numpy as np
from jax import lax
from jax.sharding import PartitionSpec as P

K = 256
GRID = 61
NG = 8

steepness = 8.0
threshold = 0.3
shift_scale = 45
HIGH = lax.Precision.HIGH


def dot(form, left, right):
    return jnp.einsum(form, left, right, precision=HIGH, preferred_element_type=jnp.float32)


def waves(left, right, length):
    turns = np.mod(np.asarray(left)[:, None] * np.asarray(right)[None, :], length)
    angles = 2.0 * math.pi * turns.astype(np.float64) / length
    return np.cos(angles), np.sin(angles)


def turned(first, second):
    return (
        first[0] * second[0] - first[1] * second[1],
        first[1] * second[0] + first[0] * second[1],
    )


def shifted_waves(count, freq, length, device, devices):
    near = np.stack(waves(np.arange(count), freq, length)).astype(np.float32)
    far = np.stack(waves(np.arange(devices) * count, freq, length)).astype(np.float32)
    far = lax.dynamic_slice_in_dim(jnp.asarray(far), device, 1, axis=1)
    return turned((far[0], far[1]), (jnp.asarray(near[0]), jnp.asarray(near[1])))


def on_device(devices, mask_field, target_print, source_points, source_groups, group_logits, pupil_radius):
    rows, n = mask_field.shape
    sources = source_points.shape[0]
    coarse = 2 * K
    step = n // coarse
    cols = coarse // devices
    half = n // 2
    device = lax.axis_index("slab")
    freq = np.arange(K, dtype=np.int64) - K // 2
    order = np.concatenate([freq[freq % 2 == 0], freq[freq % 2 == 1]])
    kh = K // 2
    norming = 1.0 / (n * n)

    cos_y, sin_y = waves(np.arange(half), order, n)
    fold = [
        jnp.asarray(np.concatenate([t[:, p * kh : (p + 1) * kh] for t in (cos_y, sin_y)], 1), jnp.float32)
        for p in (0, 1)
    ]
    lag = np.mod(np.arange(n)[None, :] - step * np.arange(coarse // 4)[:, None], n)
    kernel = np.zeros(n)
    for f in range(1, K):
        kernel += 2.0 * np.cos(2.0 * math.pi * np.mod(f * np.arange(n), n) / n)
    kernel = (kernel + 1.0) / coarse
    quarter = lax.optimization_barrier(jnp.asarray(kernel[lag], jnp.float32))
    up = jnp.concatenate([jnp.roll(quarter, i * (n // 4), axis=1) for i in range(4)], 0)
    cos_c, sin_c = waves(freq, np.arange(coarse), coarse)
    wave_x = jnp.asarray(np.concatenate([cos_c, sin_c], 1), jnp.float32)
    loc_c, loc_s = shifted_waves(rows, freq, n, device, devices)
    loc = jnp.concatenate([loc_c, loc_s], 1)
    a, b = shifted_waves(cols, order, coarse, device, devices)
    lift = jnp.concatenate([jnp.concatenate([a, -b], 1), jnp.concatenate([b, a], 1)], 0)

    cutoff = pupil_radius[0]
    shifted = (source_points - GRID // 2) * cutoff // shift_scale
    first = jnp.asarray(freq, jnp.int32)[None, None, :] + shifted[:, 0, None, None]
    second = jnp.asarray(order, jnp.int32)[None, :, None] + shifted[:, 1, None, None]
    passed = first * first + second * second <= cutoff * cutoff

    near, away = mask_field[:, :half], mask_field[:, half:]
    even = dot("xy,yq->xq", near + away, fold[0])
    odd = dot("xy,yq->xq", near - away, fold[1])
    part_c = jnp.concatenate([even[:, :kh], odd[:, :kh]], 1)
    part_s = jnp.concatenate([even[:, kh:], odd[:, kh:]], 1)
    spec = dot("xq,xk->qk", jnp.concatenate([part_c, part_s], 1), loc)
    band = jnp.concatenate(
        [spec[:K, :K] - spec[K:, K:], -(spec[:K, K:] + spec[K:, :K])], 0
    )
    band = lax.psum(band, "slab").reshape(2, K, K)

    kept = jnp.where(passed[:, None], band[None], 0.0).reshape(sources, 2 * K, K)
    wide = dot("aq,sqk->sak", lift, kept)
    both = dot("ak,kx->ax", wide.reshape(sources * 2 * cols, K), wave_x)
    both = both.reshape(sources, 2, cols, 2 * coarse)
    field_re = (both[:, 0, :, :coarse] - both[:, 1, :, coarse:]) * norming
    field_im = (both[:, 0, :, coarse:] + both[:, 1, :, :coarse]) * norming
    bright = field_re * field_re + field_im * field_im
    onehot = (source_groups[:, None] == jnp.arange(NG, dtype=jnp.int32)[None, :]).astype(jnp.float32)
    weights = jnp.exp(jnp.sum(onehot * group_logits[None, :], 1))
    total = jnp.sum(weights)
    share = weights / total
    image = jnp.sum(share[:, None, None] * bright, 0)

    tall = dot("cm,mx->cx", image, up)
    tall = lax.all_to_all(tall, "slab", 1, 0, tiled=True)
    intensity = dot("cx,cy->xy", tall, up)
    resist = jax.nn.sigmoid(steepness * (intensity - threshold))
    misfit = resist - target_print.astype(jnp.float32)
    slope = (2.0 * steepness) * misfit * resist * (1.0 - resist)
    squares = jnp.sum(misfit * misfit)
    down = dot("xy,cy->cx", slope, up)
    down = lax.all_to_all(down, "slab", 0, 1, tiled=True)
    pull = dot("cx,mx->cm", down, up)

    per_source = jnp.sum(bright * pull[None], (1, 2))
    sums = lax.psum(jnp.concatenate([per_source, squares[None]]), "slab")
    per_source, squares = sums[:-1], sums[-1]
    loss_value = (squares * norming).reshape(1)
    against = jnp.sum(share * per_source)
    source_pull = share * (per_source - against)
    group_grad = jnp.sum(onehot * source_pull[:, None], 0) * norming

    factor = (2.0 * norming) * share[:, None, None] * pull[None]
    back = jnp.stack([factor * field_re, factor * field_im], 1)
    low = dot("ax,kx->ak", back.reshape(sources * 2 * cols, coarse), wave_x[:, :coarse])
    lows = dot("ax,kx->ak", back.reshape(sources * 2 * cols, coarse), wave_x[:, coarse:])
    low = low.reshape(sources, 2, cols, K)
    lows = lows.reshape(sources, 2, cols, K)
    settle = jnp.concatenate([low[:, 0] + lows[:, 1], low[:, 1] - lows[:, 0]], 1)
    settle = dot("aq,sak->sqk", lift, settle).reshape(sources, 2, K, K)
    grad_band = jnp.sum(jnp.where(passed[:, None], settle, 0.0), 0)
    grad_band = lax.psum(grad_band.reshape(2 * K, K), "slab")

    loc_c2 = jnp.concatenate([loc_c, loc_s], 0)
    spread = dot("tk,qk->tq", loc_c2, grad_band)
    spread_re = spread[:rows, :K] - spread[rows:, K:]
    spread_im = spread[:rows, K:] + spread[rows:, :K]
    even = dot("xq,yq->xy", jnp.concatenate([spread_re[:, :kh], -spread_im[:, :kh]], 1), fold[0])
    odd = dot("xq,yq->xy", jnp.concatenate([spread_re[:, kh:], -spread_im[:, kh:]], 1), fold[1])
    mask_grad = jnp.concatenate([even + odd, even - odd], 1)
    return loss_value, mask_grad, group_grad


def solution(mesh):
    in_specs = (
        P(("clip", "slab"), None),
        P(("clip", "slab"), None),
        P("clip", None),
        P("clip"),
        P("clip"),
        P("clip"),
    )
    out_specs = (P("clip"), P(("clip", "slab"), None), P("clip"))
    return jax.shard_map(
        functools.partial(on_device, mesh.shape["slab"]),
        mesh=mesh, in_specs=in_specs, out_specs=out_specs, check_vma=False,
    )
```

```python
import functools
import math

import jax
import jax.numpy as jnp
import numpy as np
from jax import lax
from jax.sharding import PartitionSpec as P

K = 256
GRID = 61
NG = 8

steepness = 8.0
threshold = 0.3
shift_scale = 45
HIGH = lax.Precision.HIGH


def dot(form, left, right):
    return jnp.einsum(form, left, right, precision=HIGH, preferred_element_type=jnp.float32)


def waves(left, right, length):
    turns = np.mod(np.asarray(left)[:, None] * np.asarray(right)[None, :], length)
    angles = 2.0 * math.pi * turns.astype(np.float64) / length
    return np.cos(angles), np.sin(angles)


def turned(first, second):
    return (
        first[0] * second[0] - first[1] * second[1],
        first[1] * second[0] + first[0] * second[1],
    )


def shifted_waves(count, freq, length, device, devices):
    near = np.stack(waves(np.arange(count), freq, length)).astype(np.float32)
    far = np.stack(waves(np.arange(devices) * count, freq, length)).astype(np.float32)
    far = lax.dynamic_slice_in_dim(jnp.asarray(far), device, 1, axis=1)
    return turned((far[0], far[1]), (jnp.asarray(near[0]), jnp.asarray(near[1])))


def exchange(blocks):
    return lax.all_to_all(blocks, "slab", 0, 0)


def gather(block, devices):
    return lax.all_gather(block, "slab", tiled=True)


def on_device(devices, mask_field, target_print, source_points, source_groups, group_logits, pupil_radius):
    rows, n = mask_field.shape
    sources = source_points.shape[0]
    coarse = 2 * K
    step = n // coarse
    cols = coarse // devices
    half = n // 2
    device = lax.axis_index("slab")
    freq = np.arange(K, dtype=np.int64) - K // 2
    order = np.concatenate([freq[freq % 2 == 0], freq[freq % 2 == 1]])
    kh = K // 2
    norming = 1.0 / (n * n)

    cos_y, sin_y = waves(np.arange(half), order, n)
    fold = [
        jnp.asarray(np.concatenate([t[:, p * kh : (p + 1) * kh] for t in (cos_y, sin_y)], 1), jnp.float32)
        for p in (0, 1)
    ]
    lag = np.mod(np.arange(n)[None, :] - step * np.arange(coarse)[:, None], n)
    kernel = np.zeros(n)
    for f in range(1, K):
        kernel += 2.0 * np.cos(2.0 * math.pi * np.mod(f * np.arange(n), n) / n)
    kernel = (kernel + 1.0) / coarse
    up = jnp.asarray(kernel[lag], jnp.float32)
    cos_c, sin_c = waves(freq, np.arange(coarse), coarse)
    wave_x = jnp.asarray(np.concatenate([cos_c, sin_c], 1), jnp.float32)
    loc_c, loc_s = shifted_waves(rows, freq, n, device, devices)
    loc = jnp.concatenate([loc_c, loc_s], 1)
    a, b = shifted_waves(cols, order, coarse, device, devices)
    lift = jnp.concatenate([jnp.concatenate([a, -b], 1), jnp.concatenate([b, a], 1)], 0)

    cutoff = pupil_radius[0]
    shifted = (source_points - GRID // 2) * cutoff // shift_scale
    first = jnp.asarray(freq, jnp.int32)[None, None, :] + shifted[:, 0, None, None]
    second = jnp.asarray(np.tile(order, 2), jnp.int32)[None, :, None] + shifted[:, 1, None, None]
    passed = first * first + second * second <= cutoff * cutoff

    near, away = mask_field[:, :half], mask_field[:, half:]
    even = dot("xy,yq->xq", near + away, fold[0])
    odd = dot("xy,yq->xq", near - away, fold[1])
    part_c = jnp.concatenate([even[:, :kh], odd[:, :kh]], 1)
    part_s = jnp.concatenate([even[:, kh:], odd[:, kh:]], 1)
    spec = dot("xq,xk->qk", jnp.concatenate([part_c, part_s], 1), loc)
    band = jnp.concatenate(
        [spec[:K, :K] - spec[K:, K:], -(spec[:K, K:] + spec[K:, :K])], 0
    )
    band = jnp.sum(exchange(band.reshape(devices, 2 * K // devices, K)), 0)
    band = gather(band, devices)

    kept = jnp.where(passed, band[None], 0.0)
    wide = dot("aq,sqk->sak", lift, kept)
    both = dot("ak,kx->ax", wide.reshape(sources * 2 * cols, K), wave_x)
    both = both.reshape(sources, 2, cols, 2 * coarse)
    field_re = (both[:, 0, :, :coarse] - both[:, 1, :, coarse:]) * norming
    field_im = (both[:, 0, :, coarse:] + both[:, 1, :, :coarse]) * norming
    bright = field_re * field_re + field_im * field_im
    onehot = (source_groups[:, None] == jnp.arange(NG, dtype=jnp.int32)[None, :]).astype(jnp.float32)
    weights = jnp.exp(jnp.sum(onehot * group_logits[None, :], 1))
    total = jnp.sum(weights)
    share = weights / total
    image = jnp.sum(share[:, None, None] * bright, 0)

    tall = dot("cm,mx->cx", image, up)
    tall = lax.all_to_all(tall, "slab", 1, 0, tiled=True)
    intensity = dot("cx,cy->xy", tall, up)
    resist = jax.nn.sigmoid(steepness * (intensity - threshold))
    misfit = resist - target_print.astype(jnp.float32)
    slope = (2.0 * steepness) * misfit * resist * (1.0 - resist)
    squares = jnp.sum(misfit * misfit)
    down = dot("xy,cy->cx", slope, up)
    down = lax.all_to_all(down, "slab", 0, 1, tiled=True)
    pull = dot("cx,mx->cm", down, up)

    per_source = jnp.sum(bright * pull[None], (1, 2))
    sums = jnp.concatenate([per_source, squares[None]])
    factor = (2.0 * norming) * share[:, None, None] * pull[None]
    back = jnp.stack([factor * field_re, factor * field_im], 1)
    low = dot("ax,kx->ak", back.reshape(sources * 2 * cols, coarse), wave_x[:, :coarse])
    lows = dot("ax,kx->ak", back.reshape(sources * 2 * cols, coarse), wave_x[:, coarse:])
    low = low.reshape(sources, 2, cols, K)
    lows = lows.reshape(sources, 2, cols, K)
    settle = jnp.concatenate([low[:, 0] + lows[:, 1], low[:, 1] - lows[:, 0]], 1)
    settle = dot("aq,sak->sqk", lift, settle)
    grad_band = jnp.sum(jnp.where(passed, settle, 0.0), 0).reshape(devices, 2 * K // devices, K)
    extra = jnp.pad(sums[None, :], ((0, 7), (0, K - sources - 1)))
    extra = jnp.broadcast_to(extra[None], (devices, 8, K))
    grad_band = jnp.sum(exchange(jnp.concatenate([grad_band, extra], 1)), 0)
    sums = grad_band[-8, : sources + 1]
    grad_band = gather(grad_band[:-8], devices)
    per_source, squares = sums[:-1], sums[-1]
    loss_value = (squares * norming).reshape(1)
    against = jnp.sum(share * per_source)
    source_pull = share * (per_source - against)
    group_grad = jnp.sum(onehot * source_pull[:, None], 0) * norming


    loc_c2 = jnp.concatenate([loc_c, loc_s], 0)
    spread = dot("tk,qk->tq", loc_c2, grad_band)
    spread_re = spread[:rows, :K] - spread[rows:, K:]
    spread_im = spread[:rows, K:] + spread[rows:, :K]
    even = dot("xq,yq->xy", jnp.concatenate([spread_re[:, :kh], -spread_im[:, :kh]], 1), fold[0])
    odd = dot("xq,yq->xy", jnp.concatenate([spread_re[:, kh:], -spread_im[:, kh:]], 1), fold[1])
    mask_grad = jnp.concatenate([even + odd, even - odd], 1)
    return loss_value, mask_grad, group_grad


def solution(mesh):
    in_specs = (
        P(("clip", "slab"), None),
        P(("clip", "slab"), None),
        P("clip", None),
        P("clip"),
        P("clip"),
        P("clip"),
    )
    out_specs = (P("clip"), P(("clip", "slab"), None), P("clip"))
    return jax.shard_map(
        functools.partial(on_device, mesh.shape["slab"]),
        mesh=mesh, in_specs=in_specs, out_specs=out_specs, check_vma=False,
    )
```

```python
import functools
import math

import jax
import jax.numpy as jnp
import numpy as np
from jax import lax
from jax.experimental import pallas as pl
from jax.experimental.pallas import tpu as pltpu
from jax.sharding import PartitionSpec as P

K = 256
GRID = 61
NG = 8

steepness = 8.0
threshold = 0.3
shift_scale = 45
HIGH = lax.Precision.HIGH


def dot(form, left, right):
    return jnp.einsum(form, left, right, precision=HIGH, preferred_element_type=jnp.float32)


def waves(left, right, length):
    turns = np.mod(np.asarray(left)[:, None] * np.asarray(right)[None, :], length)
    angles = 2.0 * math.pi * turns.astype(np.float64) / length
    return np.cos(angles), np.sin(angles)


def turned(first, second):
    return (
        first[0] * second[0] - first[1] * second[1],
        first[1] * second[0] + first[0] * second[1],
    )


def shifted_waves(count, freq, length, device, devices):
    near = np.stack(waves(np.arange(count), freq, length)).astype(np.float32)
    far = np.stack(waves(np.arange(devices) * count, freq, length)).astype(np.float32)
    far = lax.dynamic_slice_in_dim(jnp.asarray(far), device, 1, axis=1)
    return turned((far[0], far[1]), (jnp.asarray(near[0]), jnp.asarray(near[1])))


def greet(me, devices):
    barrier = pltpu.get_barrier_semaphore()

    def signal(o, carry):
        pl.semaphore_signal(
            barrier, inc=1, device_id={"slab": lax.rem(me + o, devices)},
            device_id_type=pl.DeviceIdType.MESH,
        )
        return carry

    lax.fori_loop(1, devices, signal, 0)
    pl.semaphore_wait(barrier, devices - 1)


def spread_kernel(devices, whole, in_ref, out_ref, send_sem, recv_sem, own_sem):
    me = lax.axis_index("slab")
    mine = in_ref if whole else in_ref.at[me]
    own = pltpu.make_async_copy(mine, out_ref.at[me], own_sem)
    own.start()
    greet(me, devices)

    def transfer(o):
        peer = lax.rem(me + o, devices)
        return pltpu.make_async_remote_copy(
            src_ref=in_ref if whole else in_ref.at[peer],
            dst_ref=out_ref.at[me],
            send_sem=send_sem.at[o],
            recv_sem=recv_sem.at[o],
            device_id={"slab": peer},
            device_id_type=pl.DeviceIdType.MESH,
        )

    def start(o, carry):
        transfer(o).start()
        return carry

    def finish(o, carry):
        transfer(o).wait()
        return carry

    lax.fori_loop(1, devices, start, 0)
    own.wait()
    lax.fori_loop(1, devices, finish, 0)


def spread(block, devices, whole, number):
    shape = block.shape if not whole else (devices,) + block.shape
    return pl.pallas_call(
        functools.partial(spread_kernel, devices, whole),
        out_shape=jax.ShapeDtypeStruct(shape, block.dtype),
        in_specs=[pl.BlockSpec(memory_space=pltpu.VMEM)],
        out_specs=pl.BlockSpec(memory_space=pltpu.VMEM),
        scratch_shapes=[
            pltpu.SemaphoreType.DMA((devices,)),
            pltpu.SemaphoreType.DMA((devices,)),
            pltpu.SemaphoreType.DMA,
        ],
        compiler_params=pltpu.CompilerParams(collective_id=number, has_side_effects=True),
        name="spread%d" % number,
    )(block)


def exchange(blocks, number):
    return spread(blocks, blocks.shape[0], False, number)


def gather(block, devices, number):
    return spread(block, devices, True, number).reshape(devices * block.shape[0], block.shape[1])


def on_device(devices, mask_field, target_print, source_points, source_groups, group_logits, pupil_radius):
    rows, n = mask_field.shape
    sources = source_points.shape[0]
    coarse = 2 * K
    step = n // coarse
    cols = coarse // devices
    half = n // 2
    device = lax.axis_index("slab")
    freq = np.arange(K, dtype=np.int64) - K // 2
    order = np.concatenate([freq[freq % 2 == 0], freq[freq % 2 == 1]])
    kh = K // 2
    norming = 1.0 / (n * n)

    cos_y, sin_y = waves(np.arange(half), order, n)
    fold = [
        jnp.asarray(np.concatenate([t[:, p * kh : (p + 1) * kh] for t in (cos_y, sin_y)], 1), jnp.float32)
        for p in (0, 1)
    ]
    lag = np.mod(np.arange(n)[None, :] - step * np.arange(coarse)[:, None], n)
    kernel = np.zeros(n)
    for f in range(1, K):
        kernel += 2.0 * np.cos(2.0 * math.pi * np.mod(f * np.arange(n), n) / n)
    kernel = (kernel + 1.0) / coarse
    up = jnp.asarray(kernel[lag], jnp.float32)
    cos_c, sin_c = waves(freq, np.arange(coarse), coarse)
    wave_x = jnp.asarray(np.concatenate([cos_c, sin_c], 1), jnp.float32)
    loc_c, loc_s = shifted_waves(rows, freq, n, device, devices)
    loc = jnp.concatenate([loc_c, loc_s], 1)
    a, b = shifted_waves(cols, order, coarse, device, devices)
    lift = jnp.concatenate([jnp.concatenate([a, -b], 1), jnp.concatenate([b, a], 1)], 0)

    cutoff = pupil_radius[0]
    shifted = (source_points - GRID // 2) * cutoff // shift_scale
    first = jnp.asarray(freq, jnp.int32)[None, None, :] + shifted[:, 0, None, None]
    second = jnp.asarray(np.tile(order, 2), jnp.int32)[None, :, None] + shifted[:, 1, None, None]
    passed = first * first + second * second <= cutoff * cutoff

    near, away = mask_field[:, :half], mask_field[:, half:]
    even = dot("xy,yq->xq", near + away, fold[0])
    odd = dot("xy,yq->xq", near - away, fold[1])
    part_c = jnp.concatenate([even[:, :kh], odd[:, :kh]], 1)
    part_s = jnp.concatenate([even[:, kh:], odd[:, kh:]], 1)
    spec = dot("xq,xk->qk", jnp.concatenate([part_c, part_s], 1), loc)
    band = jnp.concatenate(
        [spec[:K, :K] - spec[K:, K:], -(spec[:K, K:] + spec[K:, :K])], 0
    )
    band = jnp.sum(exchange(band.reshape(devices, 2 * K // devices, K), 0), 0)
    band = gather(band, devices, 1)

    kept = jnp.where(passed, band[None], 0.0)
    wide = dot("aq,sqk->sak", lift, kept)
    both = dot("ak,kx->ax", wide.reshape(sources * 2 * cols, K), wave_x)
    both = both.reshape(sources, 2, cols, 2 * coarse)
    field_re = (both[:, 0, :, :coarse] - both[:, 1, :, coarse:]) * norming
    field_im = (both[:, 0, :, coarse:] + both[:, 1, :, :coarse]) * norming
    bright = field_re * field_re + field_im * field_im
    onehot = (source_groups[:, None] == jnp.arange(NG, dtype=jnp.int32)[None, :]).astype(jnp.float32)
    weights = jnp.exp(jnp.sum(onehot * group_logits[None, :], 1))
    total = jnp.sum(weights)
    share = weights / total
    image = jnp.sum(share[:, None, None] * bright, 0)

    tall = dot("cm,mx->cx", image, up)
    tall = exchange(jnp.swapaxes(tall.reshape(cols, devices, rows), 0, 1), 2).reshape(coarse, rows)
    intensity = dot("cx,cy->xy", tall, up)
    resist = jax.nn.sigmoid(steepness * (intensity - threshold))
    misfit = resist - target_print.astype(jnp.float32)
    slope = (2.0 * steepness) * misfit * resist * (1.0 - resist)
    squares = jnp.sum(misfit * misfit)
    down = dot("xy,cy->cx", slope, up)
    down = jnp.swapaxes(exchange(down.reshape(devices, cols, rows), 3), 0, 1).reshape(cols, n)
    pull = dot("cx,mx->cm", down, up)

    per_source = jnp.sum(bright * pull[None], (1, 2))
    sums = jnp.concatenate([per_source, squares[None]])
    factor = (2.0 * norming) * share[:, None, None] * pull[None]
    back = jnp.stack([factor * field_re, factor * field_im], 1)
    low = dot("ax,kx->ak", back.reshape(sources * 2 * cols, coarse), wave_x[:, :coarse])
    lows = dot("ax,kx->ak", back.reshape(sources * 2 * cols, coarse), wave_x[:, coarse:])
    low = low.reshape(sources, 2, cols, K)
    lows = lows.reshape(sources, 2, cols, K)
    settle = jnp.concatenate([low[:, 0] + lows[:, 1], low[:, 1] - lows[:, 0]], 1)
    settle = dot("aq,sak->sqk", lift, settle)
    grad_band = jnp.sum(jnp.where(passed, settle, 0.0), 0).reshape(devices, 2 * K // devices, K)
    extra = jnp.pad(sums[None, :], ((0, 7), (0, K - sources - 1)))
    extra = jnp.broadcast_to(extra[None], (devices, 8, K))
    grad_band = jnp.sum(exchange(jnp.concatenate([grad_band, extra], 1), 4), 0)
    sums = grad_band[-8, : sources + 1]
    grad_band = gather(grad_band[:-8], devices, 5)
    per_source, squares = sums[:-1], sums[-1]
    loss_value = (squares * norming).reshape(1)
    against = jnp.sum(share * per_source)
    source_pull = share * (per_source - against)
    group_grad = jnp.sum(onehot * source_pull[:, None], 0) * norming


    loc_c2 = jnp.concatenate([loc_c, loc_s], 0)
    wide_out = dot("tk,qk->tq", loc_c2, grad_band)
    spread_re = wide_out[:rows, :K] - wide_out[rows:, K:]
    spread_im = wide_out[:rows, K:] + wide_out[rows:, :K]
    even = dot("xq,yq->xy", jnp.concatenate([spread_re[:, :kh], -spread_im[:, :kh]], 1), fold[0])
    odd = dot("xq,yq->xy", jnp.concatenate([spread_re[:, kh:], -spread_im[:, kh:]], 1), fold[1])
    mask_grad = jnp.concatenate([even + odd, even - odd], 1)
    return loss_value, mask_grad, group_grad


def solution(mesh):
    in_specs = (
        P(("clip", "slab"), None),
        P(("clip", "slab"), None),
        P("clip", None),
        P("clip"),
        P("clip"),
        P("clip"),
    )
    out_specs = (P("clip"), P(("clip", "slab"), None), P("clip"))
    return jax.shard_map(
        functools.partial(on_device, mesh.shape["slab"]),
        mesh=mesh, in_specs=in_specs, out_specs=out_specs, check_vma=False,
    )
```
